32 devices in a mesh: grid: 16 (over z, y, core), orb: 2 (over x).
Axes of the slice: x: 2, y: 2, z: 4, core: 2. Of those that a mesh axis runs over, the one named last changes fastest.
Arguments:
- orbitals: float32 [32, 96, 4096], P('grid', 'orb'), may hold values from -6 to 6
- potential: float32 [32, 4096], P('grid'), may hold values from -4 to 4
- projectors: float32 [32, 256, 4096], P('grid', None, 'orb'), may hold values from -0.125 to 0.125
Outputs:
- filtered: float32 [32, 96, 4096], P('grid', 'orb')
The draws below stay inside these ranges and needn't reach their ends.
All inputs are finite; a program needn't handle non-finite values.
Results may differ from the reference program's by a relative error of at most 0.000084.
Values sent between devices are 32-bit elements; how exact they have to be, the bound alone decides.
No kernel may reach another device: no remote copies, remote signals or barrier semaphores. Data moves between devices by JAX's collectives and lax.ppermute only.
A program may use at most 128 MiB of HBM per device.

```python
import jax
import jax.numpy as jnp
from jax import lax

NX = 64
NY = 64
NPROJ = 256
NXY = 4096
NZ = 32
NORB = 96


def shard_levels(key, dims, shards, smallest, high):
    def one(axis_at, blocks):
        steps = jax.random.uniform(jax.random.fold_in(jax.random.fold_in(key, 6), axis_at), (blocks,), jnp.float32, smallest / len(shards), high / len(shards))
        return jnp.repeat(jnp.exp(steps), dims[axis_at] // blocks).reshape((-1,) + (1,) * (len(dims) - axis_at - 1))

    level = one(*shards[0])
    for cut in shards[1:]:
        level = level * one(*cut)
    return level


def scatter_about(rng, shape, width, most, pieces=(), dtype=jnp.bfloat16):
    factor_of = shard_levels(rng, shape, pieces, -0.22, 0.18) if pieces else 1.0
    result = jax.random.normal(rng, shape, jnp.float32) * width * factor_of
    return jnp.minimum(jnp.maximum(result, -most), most).astype(dtype)


def setup_inputs(seed: int = 0) -> dict:
    keys = jax.random.split(jax.random.key(seed), 4)
    orbitals = scatter_about(keys[0], (NZ, NORB, NXY), 1.0, 6.0, ((0, 16), (1, 2)), jnp.float32)
    potential = jnp.clip(jax.random.uniform(keys[1], (NZ, NXY), jnp.float32, -4.0, 4.0) * shard_levels(keys[1], (NZ, NXY), ((0, 16),), -0.4, 0.0), -4.0, 4.0)
    projectors = scatter_about(keys[2], (NZ, NPROJ, NXY), (NX * NY * NZ // 64) ** -0.5, 0.125, ((0, 16), (2, 2)), jnp.float32)
    return {"orbitals": orbitals, "potential": potential, "projectors": projectors}


grid_step = 0.5
center = 22.0
half_width = 18.0


def laplace(field):
    cube = field.reshape(field.shape[0], field.shape[1], NY, NX)
    total = -7.5 * cube
    for axis in (0, 2, 3):
        for offset, weight in ((1, 4.0 / 3.0), (2, -1.0 / 12.0)):
            total = total + weight * (jnp.roll(cube, offset, axis) + jnp.roll(cube, -offset, axis))
    return (total / (grid_step * grid_step)).reshape(field.shape)


def exchange_term(field, projectors):
    intersection = jnp.einsum("zpn,zon->po", projectors, field, precision=lax.Precision.HIGHEST)
    return -jnp.einsum("zpn,po->zon", projectors, intersection, precision=lax.Precision.HIGHEST)


def filter_step(field, potential, projectors):
    applied = -0.5 * laplace(field) + potential[:, None, :] * field + exchange_term(field, projectors)
    return (applied - center * field) / half_width


def reference(orbitals, potential, projectors):
    first = filter_step(orbitals, potential, projectors)
    return 2.0 * filter_step(first, potential, projectors) - orbitals
```

```python
import functools

import jax
import jax.numpy as jnp
from jax import lax
from jax.experimental import pallas as pl
from jax.experimental.pallas import tpu as pltpu
from jax.sharding import PartitionSpec as P

NX = 64
LANES = 128
center = 22.0
half_width = 18.0
near = -8.0 / 3.0
far = 1.0 / 6.0
middle = 15.0 - center
BOTH = ("grid", "orb")
MIB = 1 << 20

VMEM = pl.BlockSpec(memory_space=pltpu.VMEM)
SMEM = pl.BlockSpec(memory_space=pltpu.SMEM)


def sds(*shape, dtype=jnp.float32):
    return jax.ShapeDtypeStruct(shape, dtype)


def cost(flops, moved):
    return pl.CostEstimate(flops=flops, bytes_accessed=moved, transcendentals=0)


def halves(value):
    high = value.astype(jnp.bfloat16)
    low = (value - high.astype(jnp.float32)).astype(jnp.bfloat16)
    return high, low


def const_spec(shape):
    return pl.BlockSpec(shape, lambda *ids: (0,) * len(shape))


def cut_kernel(parts, where, field, potential, *outs):
    here = where[0]
    points = field.shape[2]
    width = points // parts
    for k in range(parts):
        part = lax.rem(here + k, parts)
        start = pl.multiple_of(part * width, LANES)
        before = pl.multiple_of(lax.rem(start + points - LANES, points), LANES)
        after = pl.multiple_of(lax.rem(start + width, points), LANES)
        mid, edge = outs[2 * k], outs[2 * k + 1]
        mid[...] = field[:, :, pl.ds(start, width)]
        edge[:, :, 0:LANES] = field[:, :, pl.ds(before, LANES)]
        edge[:, :, LANES : 2 * LANES] = field[:, :, pl.ds(after, LANES)]
    at = pl.ds(pl.multiple_of(here * width, LANES), width)
    for z in range(potential.shape[0]):
        outs[-1][z] = potential[z, :, at]


def cut(where, field, potential, parts):
    planes, count, points = field.shape
    width = points // parts
    shapes = [sds(planes, count, width), sds(planes, count, 2 * LANES)] * parts
    shapes.append(sds(planes, 1, width))
    outs = pl.pallas_call(
        functools.partial(cut_kernel, parts),
        out_shape=shapes,
        in_specs=[SMEM, VMEM, VMEM],
        out_specs=[VMEM] * len(shapes),
        compiler_params=pltpu.CompilerParams(vmem_limit_bytes=16 * MIB),
        cost_estimate=cost(0, 8 * field.size),
        name="cut",
    )(where, field, potential[:, None, :])
    return outs[0:-1:2], outs[1:-1:2], outs[-1]


def split_kernel(source, high, low):
    high[...], low[...] = halves(source[...])


def split(projectors):
    planes, rows, width = projectors.shape
    step = min(width, 512)
    spec = pl.BlockSpec((1, rows, step), lambda z, b: (z, 0, b))
    return pl.pallas_call(
        split_kernel,
        out_shape=[sds(planes, rows, width, dtype=jnp.bfloat16)] * 2,
        grid=(planes, width // step),
        in_specs=[spec],
        out_specs=[spec, spec],
        compiler_params=pltpu.CompilerParams(vmem_limit_bytes=16 * MIB),
        cost_estimate=cost(0, 8 * projectors.size),
        name="split",
    )(projectors)


def meet_kernel(parts, where, high, low, *refs):
    fields, (keep, give) = refs[:parts], refs[parts:]
    here, core = where[0], where[1]
    first = jnp.logical_and(pl.program_id(0) == 0, pl.program_id(1) == 0)

    @pl.when(first)
    def _():
        keep[...] = jnp.zeros_like(keep)
        give[...] = jnp.zeros_like(give)

    many = parts // 2
    nt = (((1,), (1,)), ((), ()))
    tops, bottoms = [], []
    for field in fields:
        top, bottom = halves(field[0])
        tops.append(top)
        bottoms.append(bottom)
    count = tops[0].shape[0]
    both = jnp.concatenate(tops + bottoms, axis=0)
    rows = lax.dot_general(both, high[0], nt, preferred_element_type=jnp.float32)
    more = lax.dot_general(
        jnp.concatenate(tops, axis=0), low[0], nt, preferred_element_type=jnp.float32
    )
    total = rows[: parts * count] + (rows[parts * count :] + more)
    for k in range(parts):
        owner = lax.rem(here - k + parts, parts)
        side, slot = lax.div(owner, many), lax.rem(owner, many)
        term = total[k * count : (k + 1) * count]

        @pl.when(side == core)
        def _():
            keep[slot] += term

        @pl.when(side != core)
        def _():
            give[slot] += term


def meet(where, fields, high, low):
    parts = len(fields)
    planes, count, width = fields[0].shape
    rows = high.shape[1]
    step = min(width, 1024)
    weight = pl.BlockSpec((1, rows, step), lambda z, b: (z, 0, b))
    field = pl.BlockSpec((1, count, step), lambda z, b: (z, 0, b))
    shape = (parts // 2, count, rows)
    return pl.pallas_call(
        functools.partial(meet_kernel, parts),
        out_shape=[sds(*shape)] * 2,
        grid=(planes, width // step),
        in_specs=[SMEM, weight, weight] + [field] * parts,
        out_specs=[const_spec(shape)] * 2,
        compiler_params=pltpu.CompilerParams(vmem_limit_bytes=20 * MIB),
        cost_estimate=cost(6 * parts * count * rows * planes * width, 4 * high.size),
        name="meet",
    )(where, high, low, *fields)


def over_devices(keep, give):
    grid, orb = lax.axis_size("grid"), lax.axis_size("orb")
    swap = [(i, i ^ 1) for i in range(grid)]
    value = keep + lax.ppermute(give, "grid", swap)
    bits = [(1 << i, 0) for i in range(1, grid.bit_length() - 1)]
    bits[1:1] = [(0, 1 << i) for i in range(orb.bit_length() - 1)]
    while bits:
        group, bits = bits[:2], bits[2:]
        flips = list(group)
        if len(group) == 2:
            flips.append((group[0][0] ^ group[1][0], group[0][1] ^ group[1][1]))
        terms = [value]
        for g_flip, o_flip in flips:
            pairs = [
                (g * orb + o, (g ^ g_flip) * orb + (o ^ o_flip))
                for g in range(grid)
                for o in range(orb)
            ]
            terms.append(lax.ppermute(value, BOTH, pairs))
        while len(terms) > 1:
            terms = [sum(terms[i : i + 2]) for i in range(0, len(terms), 2)]
        value = terms[0]
    return value, lax.ppermute(value, "grid", swap)


def apply_kernel(chunk, parts, last, where, mid, edge, below, above, potential, high, low, mine, other, *rest):
    if last:
        origin, out, wide = rest
    else:
        out, rim, wide = rest
    b = pl.program_id(0)
    planes, count, width = mid.shape
    step = out.shape[2]
    columns = step // LANES
    many = parts // 2
    owner = lax.rem(where[0] - chunk + parts, parts)
    side, slot = lax.div(owner, many), lax.rem(owner, many)

    @pl.when(b == 0)
    def _():
        wide[:, :, 0:LANES] = edge[:, :, 0:LANES]
        wide[:, :, LANES : LANES + width] = mid[...]
        wide[:, :, LANES + width :] = edge[:, :, LANES:]

    factor = jnp.where(side == where[1], mine[slot], other[slot])
    top, bottom = halves(factor)
    both = jnp.concatenate([top, bottom], axis=0)
    nn = (((1,), (0,)), ((), ()))
    x = lax.broadcasted_iota(jnp.int32, (count, LANES), 1)
    lower = x < NX
    x = x & (NX - 1)

    def column(j):
        return pl.ds(pl.multiple_of(b * step + j * LANES, LANES), LANES)

    def turned(value, shift):
        return pltpu.roll(value, shift, axis=1)

    for z in range(planes):
        rows = lax.dot_general(both, high[z], nn, preferred_element_type=jnp.float32)
        more = lax.dot_general(top, low[z], nn, preferred_element_type=jnp.float32)
        drawn = rows[:count] + (rows[count:] + more)
        blocks = [wide[z, :, column(j)] for j in range(columns + 2)]
        swapped = [turned(block, NX) for block in blocks]
        for j in range(columns):
            here, back = blocks[j + 1], swapped[j + 1]

            def plane(offset):
                if z + offset < 0:
                    return below[2 + z + offset, :, column(j)]
                if z + offset >= planes:
                    return above[z + offset - planes, :, column(j)]
                return mid[z + offset, :, column(j)]

            one = jnp.where(lower, swapped[j], back) + jnp.where(lower, back, swapped[j + 2])
            one += turned(jnp.where(x == NX - 1, back, here), 1)
            one += turned(jnp.where(x == 0, back, here), LANES - 1)
            one += plane(-1) + plane(1)
            two = blocks[j] + blocks[j + 2]
            two += turned(jnp.where(x >= NX - 2, back, here), 2)
            two += turned(jnp.where(x <= 1, back, here), LANES - 2)
            two += plane(-2) + plane(2)
            span = slice(j * LANES, (j + 1) * LANES)
            level = potential[z, :, column(j)] + middle
            value = level * here + near * one + far * two - drawn[:, span]
            value = value * (1.0 / half_width)
            if last:
                out[z, :, span] = 2.0 * value - origin[z, :, span]
                continue
            out[z, :, span] = value
            if j == columns - 1:

                @pl.when(b == pl.num_programs(0) - 1)
                def _():
                    rim[z, :, 0:LANES] = value

            if j == 0:

                @pl.when(b == 0)
                def _():
                    rim[z, :, LANES : 2 * LANES] = value


def apply(where, chunk, parts, mid, edge, below, above, potential, high, low, mine, other, origin=None):
    planes, count, width = mid.shape
    rows = high.shape[1]
    step = min(width, 512)
    weight = pl.BlockSpec((planes, rows, step), lambda b: (0, 0, b))
    part = pl.BlockSpec((planes, count, step), lambda b: (0, 0, b))
    operands = [where, mid, edge, below, above, potential, high, low, mine, other]
    specs = [SMEM] + [const_spec(v.shape) for v in operands[1:6]]
    specs += [weight, weight, const_spec(mine.shape), const_spec(other.shape)]
    shapes, outs = [sds(planes, count, width)], [part]
    last = origin is not None
    if last:
        operands.append(origin)
        specs.append(part)
    else:
        shapes.append(sds(planes, count, 2 * LANES))
        outs.append(const_spec((planes, count, 2 * LANES)))
    result = pl.pallas_call(
        functools.partial(apply_kernel, chunk, parts, last),
        out_shape=shapes,
        grid=(width // step,),
        in_specs=specs,
        out_specs=outs,
        scratch_shapes=[pltpu.VMEM((planes, count, width + 2 * LANES), jnp.float32)],
        compiler_params=pltpu.CompilerParams(vmem_limit_bytes=24 * MIB),
        cost_estimate=cost(6 * count * rows * planes * width, 4 * high.size + 20 * mid.size),
        name="final" if last else "first",
    )(*operands)
    return result[0] if last else result


def join_kernel(where, *refs):
    parts, out = refs[:-1], refs[-1]
    for k, part in enumerate(parts):

        @pl.when(pl.program_id(0) == k)
        def _():
            out[...] = part[...]


def join(where, pieces):
    parts = len(pieces)
    planes, count, width = pieces[0].shape
    return pl.pallas_call(
        join_kernel,
        out_shape=sds(planes, count, parts * width),
        grid_spec=pltpu.PrefetchScalarGridSpec(
            num_scalar_prefetch=1,
            grid=(parts,),
            in_specs=[pl.BlockSpec((planes, count, width), lambda k, w: (0, 0, 0))] * parts,
            out_specs=pl.BlockSpec(
                (planes, count, width), lambda k, w: (0, 0, lax.rem(w[0] + k, parts))
            ),
        ),
        compiler_params=pltpu.CompilerParams(vmem_limit_bytes=24 * MIB),
        cost_estimate=cost(0, 8 * parts * pieces[0].size),
        name="join",
    )(where, *pieces)


def shifted(value, axis, shift):
    size = lax.axis_size(axis)
    return lax.ppermute(value, axis, [(i, (i + shift) % size) for i in range(size)])


def shards(orbitals, potential, projectors):
    parts = lax.axis_size("orb")
    where = jnp.stack([lax.axis_index("orb"), lax.axis_index("grid") % 2]).astype(jnp.int32)
    mids, edges, level = cut(where, orbitals, potential, parts)
    fields = [mids[0]] + [shifted(mids[k], "orb", k) for k in range(1, parts)]
    edges = [edges[0]] + [shifted(edges[k], "orb", k) for k in range(1, parts)]
    high, low = split(projectors)

    def neighbours(field):
        return shifted(field[-2:], "grid", 1), shifted(field[:2], "grid", -1)

    around = [neighbours(field) for field in fields]
    mine, other = over_devices(*meet(where, fields, high, low))
    firsts, rims = [None] * parts, [None] * parts
    for k in reversed(range(parts)):
        firsts[k], rims[k] = apply(
            where, k, parts, fields[k], edges[k], *around[k], level, high, low, mine, other
        )
    around = [neighbours(field) for field in firsts]
    borders = []
    for k in range(parts):
        if parts == 2:
            borders.append(shifted(rims[1 - k], "orb", 1))
        else:
            lower = shifted(rims[(k - 1) % parts][:, :, :LANES], "orb", 1)
            upper = shifted(rims[(k + 1) % parts][:, :, LANES:], "orb", -1)
            borders.append(jnp.concatenate([lower, upper], axis=2))
    mine, other = over_devices(*meet(where, firsts, high, low))
    outs = [None] * parts
    for k in reversed(range(parts)):
        outs[k] = apply(
            where, k, parts, firsts[k], borders[k], *around[k], level, high, low, mine, other,
            origin=fields[k],
        )
        if k:
            outs[k] = shifted(outs[k], "orb", -k)
    return join(where, outs)


def solution(mesh):
    placed = (P("grid", "orb", None), P("grid", None), P("grid", None, "orb"))
    return jax.shard_map(
        shards, mesh=mesh, in_specs=placed, out_specs=P("grid", "orb", None), check_vma=False
    )
```

```python
import functools

import jax
import jax.numpy as jnp
from jax import lax
from jax.experimental import pallas as pl
from jax.experimental.pallas import tpu as pltpu
from jax.sharding import PartitionSpec as P


NX = 64
LANES = 128
center = 22.0
half_width = 18.0
near = -8.0 / 3.0
far = 1.0 / 6.0
middle = 15.0 - center
BOTH = ("grid", "orb")
MIB = 1 << 20


VMEM = pl.BlockSpec(memory_space=pltpu.VMEM)
SMEM = pl.BlockSpec(memory_space=pltpu.SMEM)
ANY = pl.BlockSpec(memory_space=pl.ANY)


def sds(*shape, dtype=jnp.float32):
    return jax.ShapeDtypeStruct(shape, dtype)


def cost(flops, moved):
    return pl.CostEstimate(flops=flops, bytes_accessed=moved, transcendentals=0)


def halves(value):
    high = value.astype(jnp.bfloat16)
    low = (value - high.astype(jnp.float32)).astype(jnp.bfloat16)
    return high, low


def dot(left, right, contract):
    return lax.dot_general(left, right, (contract, ((), ())), preferred_element_type=jnp.float32)


def call(kernel, shapes, operands, specs, estimate, scratch=()):
    return pl.pallas_call(
        kernel,
        out_shape=shapes,
        in_specs=specs,
        out_specs=[VMEM] * len(shapes),
        scratch_shapes=list(scratch),
        compiler_params=pltpu.CompilerParams(vmem_limit_bytes=24 * MIB),
        cost_estimate=estimate,
    )(*operands)


def cut_kernel(parts, facts, field, potential, *refs):
    outs, sem = refs[:-1], refs[-1]
    here = facts[0]
    points = field.shape[2]
    width = points // parts
    copies = []

    def fetch(start, size, target):
        at = pl.ds(pl.multiple_of(start, LANES), size)
        copies.append(pltpu.make_async_copy(field.at[:, :, at], target, sem.at[len(copies)]))

    for k in reversed(range(parts)):
        start = lax.rem(here + k, parts) * width
        mid, edge = outs[2 * k], outs[2 * k + 1]
        fetch(start, width, mid)
        fetch(lax.rem(start + points - LANES, points), LANES, edge.at[:, :, 0:LANES])
        fetch(lax.rem(start + width, points), LANES, edge.at[:, :, LANES:])
    for copy in copies:
        copy.start()
    at = pl.ds(pl.multiple_of(here * width, LANES), width)
    outs[-1][...] = potential[:, at] + middle
    for copy in copies:
        copy.wait()


def cut(facts, field, potential, parts):
    planes, count, points = field.shape
    width = points // parts
    shapes = [sds(planes, count, width), sds(planes, count, 2 * LANES)] * parts
    shapes.append(sds(planes, width))
    outs = call(
        functools.partial(cut_kernel, parts), shapes, (facts, field, potential),
        [SMEM, ANY, VMEM], cost(0, 8 * field.size), [pltpu.SemaphoreType.DMA((3 * parts,))],
    )
    return outs[0:-1:2], outs[1:-1:2], outs[-1]


def split_kernel(source, high, low):
    high[...], low[...] = halves(source[...])


def split(projectors):
    planes, rows, width = projectors.shape
    step = min(width, 512)
    spec = pl.BlockSpec((1, rows, step), lambda z, b: (z, 0, b))
    return pl.pallas_call(
        split_kernel,
        out_shape=[sds(planes, rows, width, dtype=jnp.bfloat16)] * 2,
        grid=(planes, width // step),
        in_specs=[spec],
        out_specs=[spec, spec],
        compiler_params=pltpu.CompilerParams(vmem_limit_bytes=16 * MIB),
        cost_estimate=cost(0, 8 * projectors.size),
        name="split",
    )(projectors)


def overlap(values, high, low):
    tops, bottoms = zip(*[halves(value) for value in values])
    rows = dot(jnp.concatenate(tops + bottoms, axis=0), high, ((1,), (1,)))
    more = dot(jnp.concatenate(tops, axis=0), low, ((1,), (1,)))
    size = more.shape[0]
    return rows[:size] + (rows[size:] + more)


def hand_out(facts, parts, total, keep, give):
    count, half = keep.shape[1], parts // 2
    for k in range(parts):
        owner = lax.rem(facts[0] - k + parts, parts)
        side, slot = lax.div(owner, half), lax.rem(owner, half)

        @pl.when(side == facts[1])
        def _():
            keep[slot] = total[k * count : (k + 1) * count, :]

        @pl.when(side != facts[1])
        def _():
            give[slot] = total[k * count : (k + 1) * count, :]


def meet_kernel(parts, facts, high, low, *refs):
    fields, (keep, give, total) = refs[:parts], refs[parts:]
    planes, _, width = fields[0].shape
    step = min(width, 1024)
    for z in range(planes):
        for b in range(width // step):
            at = slice(b * step, (b + 1) * step)
            term = overlap([f[z, :, at] for f in fields], high[z, :, at], low[z, :, at])
            if z == 0 and b == 0:
                total[...] = term
            else:
                total[...] += term
    hand_out(facts, parts, total, keep, give)


def meet(facts, fields, high, low):
    parts = len(fields)
    planes, count, width = fields[0].shape
    rows = high.shape[1]
    return call(
        functools.partial(meet_kernel, parts), [sds(parts // 2, count, rows)] * 2,
        (facts, high, low, *fields), [SMEM] + [VMEM] * (2 + parts),
        cost(6 * parts * count * rows * planes * width, 4 * high.size),
        [pltpu.VMEM((parts * count, rows), jnp.float32)],
    )


def flat_pairs(grid, orb, target):
    pairs = []
    for g in range(grid):
        for o in range(orb):
            to = target(g, o)
            if to is not None:
                pairs.append((g * orb + o, to[0] * orb + to[1]))
    return pairs


def over_devices(keep, give):
    grid, orb = lax.axis_size("grid"), lax.axis_size("orb")

    def send(value, flips):
        def target(g, o):
            for axis, flip in flips:
                g, o = (g ^ flip, o) if axis == "grid" else (g, o ^ flip)
            return g, o

        return lax.ppermute(value, BOTH, flat_pairs(grid, orb, target))

    core = [("grid", 1)]
    value = keep + send(give, core)
    flips = [("grid", 1 << i) for i in range(1, grid.bit_length() - 1)]
    flips[1:1] = [("orb", 1 << i) for i in range(orb.bit_length() - 1)]
    while flips:
        group, flips = flips[:2], flips[2:]
        routes = [[flip] for flip in group] + ([group] if len(group) == 2 else [])
        terms = [value] + [send(value, route) for route in routes]
        while len(terms) > 1:
            terms = [sum(terms[i : i + 2]) for i in range(0, len(terms), 2)]
        value = terms[0]
    return value, send(value, core)


def apply_kernel(chunks, parts, last, facts, level, high, low, mine, other, *refs):
    many = len(chunks)
    inputs, refs = refs[: 4 * many], refs[4 * many :]
    if last:
        origins, refs = refs[:many], refs[many:]
    outs, refs = refs[:many], refs[many:]
    if not last:
        rims, (keep, give, total), refs = refs[:many], refs[many : many + 3], refs[many + 3 :]
    wides = refs
    planes, count, width = outs[0].shape
    step = min(width, 512)
    columns = step // LANES
    half = parts // 2

    factors = []
    for i, chunk in enumerate(chunks):
        mid, edge = inputs[4 * i], inputs[4 * i + 1]
        wides[i][:, :, 0:LANES] = edge[:, :, 0:LANES]
        wides[i][:, :, LANES : LANES + width] = mid[...]
        wides[i][:, :, LANES + width :] = edge[:, :, LANES:]
        owner = lax.rem(facts[0] - chunk + parts, parts)
        side, slot = lax.div(owner, half), lax.rem(owner, half)
        factors.append(jnp.where(side == facts[1], mine[slot], other[slot]))
    top, bottom = halves(jnp.concatenate(factors, axis=0))
    both = jnp.concatenate([top, bottom], axis=0)
    size = many * count
    x = lax.broadcasted_iota(jnp.int32, (count, LANES), 1)
    lower = x < NX
    x = x & (NX - 1)

    def turned(value, shift):
        return pltpu.roll(value, shift, axis=1)

    if not last:
        total[...] = jnp.zeros_like(total)

    def block(b, carry):
        def column(j):
            return pl.ds(pl.multiple_of(b * step + j * LANES, LANES), LANES)

        at = pl.ds(pl.multiple_of(b * step, LANES), step)
        for z in range(planes):
            rows = dot(both, high[z, :, at], ((1,), (0,)))
            more = dot(top, low[z, :, at], ((1,), (0,)))
            drawn = rows[:size] + (rows[size:] + more)
            for i in range(many):
                mid, _, below, above = inputs[4 * i : 4 * i + 4]
                wide = wides[i]
                blocks = [wide[z, :, column(j)] for j in range(columns + 2)]
                swapped = [turned(value, NX) for value in blocks]
                for j in range(columns):
                    here, back = blocks[j + 1], swapped[j + 1]
                    where = column(j)

                    def plane(offset):
                        to = z + offset
                        if to < 0:
                            return below[2 + to, :, where]
                        if to >= planes:
                            return above[to - planes, :, where]
                        return mid[to, :, where]

                    one = jnp.where(lower, swapped[j], back) + jnp.where(lower, back, swapped[j + 2])
                    one += turned(jnp.where(x == NX - 1, back, here), 1)
                    one += turned(jnp.where(x == 0, back, here), LANES - 1)
                    one += plane(-1) + plane(1)
                    two = blocks[j] + blocks[j + 2]
                    two += turned(jnp.where(x >= NX - 2, back, here), 2)
                    two += turned(jnp.where(x <= 1, back, here), LANES - 2)
                    two += plane(-2) + plane(2)
                    value = level[z : z + 1, where] * here + near * one + far * two
                    value -= drawn[i * count : (i + 1) * count, j * LANES : (j + 1) * LANES]
                    value = value * (1.0 / half_width)
                    if last:
                        value = 2.0 * value - origins[i][z, :, where]
                    outs[i][z, :, where] = value
            if not last:
                total[...] += overlap([out[z, :, at] for out in outs], high[z, :, at], low[z, :, at])
        return carry

    lax.fori_loop(0, width // step, block, 0)
    if not last:
        hand_out(facts, parts, total, keep, give)
        for i in range(many):
            rims[i][:, :, 0:LANES] = outs[i][:, :, width - LANES :]
            rims[i][:, :, LANES:] = outs[i][:, :, 0:LANES]


def apply(facts, level, high, low, mine, other, chunks, parts, inputs, origins=None):
    planes, count, width = inputs[0][0].shape
    rows = high.shape[1]
    many = len(chunks)
    operands = [facts, level, high, low, mine, other]
    for group in inputs:
        operands += group
    last = origins is not None
    shapes = [sds(planes, count, width)] * many
    scratch = [pltpu.VMEM((planes, count, width + 2 * LANES), jnp.float32)] * many
    if last:
        operands += origins
    else:
        shapes = shapes + [sds(planes, count, 2 * LANES)] * many
        shapes += [sds(parts // 2, count, rows)] * 2
        scratch = [pltpu.VMEM((many * count, rows), jnp.float32)] + scratch
    work = 6 * many * count * rows * planes * width
    return call(
        functools.partial(apply_kernel, chunks, parts, last),
        shapes, operands, [SMEM] + [VMEM] * (len(operands) - 1),
        cost(work if last else 2 * work, 4 * high.size + 24 * many * inputs[0][0].size), scratch,
    )


def join_kernel(parts, facts, *refs):
    pieces, out, sem = refs[:parts], refs[parts], refs[parts + 1]
    width = pieces[0].shape[2]
    copies = []
    for k, piece in enumerate(pieces):
        at = pl.ds(pl.multiple_of(lax.rem(facts[0] + k, parts) * width, LANES), width)
        copies.append(pltpu.make_async_copy(piece, out.at[:, :, at], sem.at[k]))
    for copy in copies:
        copy.start()
    for copy in copies:
        copy.wait()


def join(facts, pieces):
    parts = len(pieces)
    planes, count, width = pieces[0].shape
    return pl.pallas_call(
        functools.partial(join_kernel, parts),
        out_shape=sds(planes, count, parts * width),
        in_specs=[SMEM] + [VMEM] * parts,
        out_specs=ANY,
        scratch_shapes=[pltpu.SemaphoreType.DMA((parts,))],
        compiler_params=pltpu.CompilerParams(vmem_limit_bytes=16 * MIB),
        cost_estimate=cost(0, 8 * parts * pieces[0].size),
        name="join",
    )(facts, *pieces)


def shifted(value, axis, shift):
    size = lax.axis_size(axis)
    return lax.ppermute(value, axis, [(i, (i + shift) % size) for i in range(size)])


def neighbours(field):
    return [shifted(field[-2:], "grid", 1), shifted(field[:2], "grid", -1)]


def shards(orbitals, potential, projectors):
    parts = lax.axis_size("orb")
    place = lax.axis_index("grid")
    facts = jnp.stack([lax.axis_index("orb"), place & 1]).astype(jnp.int32)
    mids, edges, level = cut(facts, orbitals, potential, parts)
    fields = [mids[0]] + [shifted(mids[k], "orb", k) for k in range(1, parts)]
    edges = [edges[0]] + [shifted(edges[k], "orb", k) for k in range(1, parts)]
    high, low = split(projectors)
    around = [neighbours(field) for field in fields]
    mine, other = over_devices(*meet(facts, fields, high, low))
    inputs = [[fields[k], edges[k]] + around[k] for k in range(parts)]
    result = apply(facts, level, high, low, mine, other, tuple(range(parts)), parts, inputs)
    firsts, rims, shares = result[:parts], result[parts:-2], result[-2:]
    around = [neighbours(field) for field in firsts]
    borders = []
    for k in range(parts):
        if parts == 2:
            borders.append(shifted(rims[1 - k], "orb", 1))
        else:
            lower = shifted(rims[(k - 1) % parts][:, :, :LANES], "orb", 1)
            upper = shifted(rims[(k + 1) % parts][:, :, LANES:], "orb", -1)
            borders.append(jnp.concatenate([lower, upper], axis=2))
    mine, other = over_devices(*shares)
    outs = [None] * parts
    for k in reversed(range(parts)):
        group = [[firsts[k], borders[k]] + around[k]]
        outs[k] = apply(facts, level, high, low, mine, other, (k,), parts, group, [fields[k]])[0]
        if k:
            outs[k] = shifted(outs[k], "orb", -k)
    return join(facts, outs)


def solution(mesh):
    placed = (P("grid", "orb", None), P("grid", None), P("grid", None, "orb"))

    step = jax.shard_map(
        shards, mesh=mesh, in_specs=placed, out_specs=P("grid", "orb", None), check_vma=False
    )
    if dict(mesh.shape)["orb"] != 2:
        return step
    return step
```
